256 devices in a mesh: shift: 8 (over y_lo, x), sub: 32 (over y_hi, z, core).
Axes of the slice: x: 4, y: 4 (y_hi: 2, y_lo: 2; y = y_hi * 2 + y_lo), z: 8, core: 2. Of those that a mesh axis runs over, the one named last changes fastest.
Arguments:
- interior_rhs: bfloat16 [32, 1024, 384], P('sub'), may hold values from -6 to 6
- interface_rhs: bfloat16 [2048, 384], replicated, may hold values from -6 to 6
- interior_inverse: bfloat16 [16, 32, 1024, 1024], P('shift', 'sub'), may hold values from -0.1875 to 0.1875
- coupling: bfloat16 [32, 1024, 256], P('sub'), may hold values from -0.1875 to 0.1875
- schur_inverse: bfloat16 [16, 2048, 2048], P('shift', 'sub'), may hold values from -0.125 to 0.125
- weights: float32 [16], P('shift'), may hold values from -1 to 1
- owner_sub: int32 [32], replicated, may hold values from 0 to 31, each once
- index_blocks: int32 [32, 256], replicated, may hold values from 0 to 2047, as said below
Outputs:
- filtered: float32 [1024, 32, 384], P('shift', 'sub')
The draws below stay inside these ranges and needn't reach their ends.
Inputs may be any that keep to these rules, and one draw needn't show every extreme that they name: `index_blocks`: each row holds 256 distinct interface unknowns; of each aligned block of 2048 // 32 interface unknowns a row holds at most 16, and exactly 16 of some block. `owner_sub`: each position names a different substructure.
All inputs are finite; a program needn't handle non-finite values.
Results may differ from the reference program's by a relative error of at most 0.0053.
Values may be sent and summed in bfloat16 or wider, within the bound.
No kernel may reach another device: no remote copies, remote signals or barrier semaphores. Data moves between devices by JAX's collectives and lax.ppermute only.
A program may use at most 64 MiB of HBM per device.

```python
import jax
import jax.numpy as jnp
from jax import lax

NI = 1024
NG = 2048
NGL = 256
COLS = 384
SHIFTS = 16
SUBS = 32
MOST = 16


def draw_index_blocks(key, part):
    block = NG // SUBS
    keys = jax.random.split(jax.random.fold_in(key, 7), SUBS)

    def one_row(single):
        first, second, third, fourth = jax.random.split(single, 4)
        full = jax.random.randint(first, (), 0, SUBS).astype(jnp.int32)
        others = jax.random.permutation(second, (SUBS - 1) * MOST)[:NGL - MOST].astype(jnp.int32)
        others = jnp.where(others >= full * MOST, others + MOST, others)
        slots = jnp.concatenate([full * MOST + jnp.arange(MOST, dtype=jnp.int32), others])
        orders = jax.vmap(lambda inner: jax.random.permutation(inner, block).astype(jnp.int32))(jax.random.split(third, SUBS))
        group = slots // MOST
        within = slots % MOST
        rows = group * block + orders[group, within]
        return rows[jax.random.permutation(fourth, NGL)]
    return jax.vmap(one_row)(keys).astype(jnp.int32)


def block_levels(own_key, extent, pieces, low, largest):
    level = 1.0
    for position, parts in pieces:
        heights = jax.random.uniform(jax.random.fold_in(jax.random.fold_in(own_key, 6), position), (parts,), jnp.float32, low / len(pieces), largest / len(pieces))
        level = level * jnp.repeat(jnp.exp(heights), extent[position] // parts).reshape((-1,) + (1,) * (len(extent) - 1 - position))
    return level


def normal_values(rng, extent, scale, reach, cuts=(), kind=jnp.bfloat16):
    array = scale * jax.random.normal(rng, extent, jnp.float32)
    if cuts:
        array = array * block_levels(rng, extent, cuts, -0.22, 0.18)
    return jnp.clip(array, -reach, reach).astype(kind)


def setup_inputs(seed: int = 0) -> dict:
    seeds = jax.random.split(jax.random.key(seed), 9)
    interior_rhs = normal_values(seeds[0], (SUBS, NI, COLS), 1.0, 6.0, ((0, 32),))
    interface_rhs = normal_values(seeds[1], (NG, COLS), 1.0, 6.0)
    interior_inverse = normal_values(seeds[2], (SHIFTS, SUBS, NI, NI), NI ** -0.5, 0.1875, ((0, 8), (1, 32)))
    coupling = normal_values(seeds[3], (SUBS, NI, NGL), NI ** -0.5, 0.1875, ((0, 32),))
    schur_inverse = normal_values(seeds[4], (SHIFTS, NG, NG), NG ** -0.5, 0.125, ((0, 8), (1, 32)))
    weights = jnp.clip(jax.random.uniform(seeds[5], (SHIFTS,), jnp.float32, -1.0, 1.0) * block_levels(seeds[5], (SHIFTS,), ((0, 8),), -0.4, 0.0), -1.0, 1.0)
    owner_sub = jax.random.permutation(seeds[6], SUBS).astype(jnp.int32)
    index_blocks = draw_index_blocks(jax.random.fold_in(seeds[8], 71), 0)
    return dict(interior_rhs=interior_rhs, interface_rhs=interface_rhs, interior_inverse=interior_inverse, coupling=coupling, schur_inverse=schur_inverse, weights=weights, owner_sub=owner_sub, index_blocks=index_blocks)


def reference(interior_rhs, interface_rhs, interior_inverse, coupling, schur_inverse, weights, owner_sub, index_blocks):
    idx = index_blocks[owner_sub]
    flat_idx = idx.reshape(-1)
    rhs_f = interior_rhs.astype(jnp.float32)
    coup_f = coupling.astype(jnp.float32)

    def one_shift(args):
        inverse, schur, weight = args
        inv_f = inverse.astype(jnp.float32)
        eliminated = jnp.einsum("sij,sjc->sic", inv_f, rhs_f).astype(jnp.bfloat16)
        coupled = jnp.einsum("sik,sic->skc", coup_f, eliminated.astype(jnp.float32)).astype(jnp.bfloat16)
        placed = jnp.zeros((NG, COLS), jnp.float32).at[flat_idx].add(coupled.reshape(-1, COLS).astype(jnp.float32))
        reduced = (interface_rhs.astype(jnp.float32) - placed).astype(jnp.bfloat16)
        interface_sol = jnp.dot(schur, reduced, preferred_element_type=jnp.float32).astype(jnp.bfloat16)
        picked = interface_sol[idx]
        correction = jnp.einsum("sik,skc->sic", coup_f, picked.astype(jnp.float32)).astype(jnp.bfloat16)
        interior_sol = eliminated.astype(jnp.float32) - jnp.einsum("sij,sjc->sic", inv_f, correction.astype(jnp.float32))
        return weight * interior_sol

    terms = lax.map(one_shift, (interior_inverse, schur_inverse, weights))
    accumulated = jnp.sum(terms, axis=0)
    return jnp.transpose(accumulated, (1, 0, 2))
```

```python
import jax
import jax.numpy as jnp
from jax import lax
from jax.sharding import Mesh, PartitionSpec as P

BF = jnp.bfloat16
F32 = jnp.float32
SUB = ("yh", "z", "c")
CHIPS = ("yh", "z")
SHIFT = ("yl", "x")


def dot(a, b):
    return jnp.dot(a, b, preferred_element_type=F32)


def on_device(
    interior_rhs,
    interface_rhs,
    interior_inverse,
    coupling,
    schur_inverse,
    weights,
    owner_sub,
    index_blocks,
):
    core = lax.axis_index("c")
    chip = lax.axis_index(CHIPS)
    first = core == 0
    swap = [(0, 1), (1, 0)]
    rhs = interior_rhs[0]
    couple = coupling[0]

    schur_keep = jnp.where(first, schur_inverse[0], schur_inverse[1])
    schur_give = jnp.where(first, schur_inverse[1], schur_inverse[0])
    schur_got = lax.ppermute(schur_give, "c", swap)
    schur = jnp.concatenate(
        [jnp.where(first, schur_keep, schur_got), jnp.where(first, schur_got, schur_keep)], axis=0
    )

    names = lax.broadcasted_iota(jnp.int32, (32, 32, 1), 1)
    idx_all = jnp.sum(
        jnp.where(owner_sub[:, None, None] == names, index_blocks[None], 0), axis=1
    )

    def packer(position):
        idx = lax.dynamic_index_in_dim(idx_all, position, 0, keepdims=False)
        mine, other = idx[:, None], idx[None, :]
        rank = jnp.sum(((mine // 64 == other // 64) & (other < mine)).astype(jnp.int32), axis=1)
        slot = (idx // 64) * 16 + rank
        return (lax.broadcasted_iota(jnp.int32, (512, 256), 0) == slot[None, :]).astype(BF)

    pack = [packer(2 * chip), packer(2 * chip + 1)]

    rows = lax.broadcasted_iota(jnp.int32, (1, 1, 128), 2) + 128 * chip
    held = jnp.any(idx_all[:, :, None] == rows, axis=1)
    low = lax.broadcasted_iota(jnp.int32, (128, 128), 0)
    high = lax.broadcasted_iota(jnp.int32, (128, 128), 1)
    before = ((low < high) & (low // 64 == high // 64)).astype(BF)
    place = dot(held.astype(BF), before).astype(jnp.int32)
    place = place + 16 * (lax.broadcasted_iota(jnp.int32, (32, 128), 1) // 64)
    place = jnp.where(held, place, -1)
    select = (
        (place[:, None, :] == lax.broadcasted_iota(jnp.int32, (32, 32, 128), 1))
        .astype(BF)
        .reshape(1024, 128)
    )

    eliminated = [dot(interior_inverse[j, 0], rhs).astype(BF) for j in range(2)]
    coupled = [
        lax.dot_general(couple, e, (((0,), (0,)), ((), ())), preferred_element_type=F32).astype(BF)
        for e in eliminated
    ]
    keep = jnp.where(first, coupled[0], coupled[1])
    give = jnp.where(first, coupled[1], coupled[0])
    got = lax.ppermute(give, "c", swap)
    of_chip = [jnp.where(first, keep, got), jnp.where(first, got, keep)]
    packed = jnp.concatenate(
        [dot(pack[i], of_chip[i]).astype(BF).reshape(16, 32, 384) for i in range(2)], axis=1
    )
    arrived = lax.all_to_all(packed, CHIPS, 0, 0, tiled=True).reshape(1024, 384)
    summed = lax.dot_general(
        select, arrived, (((0,), (0,)), ((), ())), preferred_element_type=F32
    )
    own_rows = lax.dynamic_slice_in_dim(interface_rhs, 128 * chip, 128, 0)
    reduced = (own_rows.astype(F32) - summed).astype(BF)
    everywhere = lax.all_to_all(
        jnp.broadcast_to(reduced[None], (16, 128, 384)), CHIPS, 0, 0, tiled=True
    ).reshape(2048, 384)
    solved = dot(schur, everywhere).astype(BF)
    answers = dot(select, solved).astype(BF).reshape(16, 64, 384)
    back = lax.all_to_all(answers, CHIPS, 0, 0, tiled=True).reshape(16, 2, 32, 384)
    picked = [
        lax.dot_general(
            pack[i],
            back[:, i].reshape(512, 384),
            (((0,), (0,)), ((), ())),
            preferred_element_type=F32,
        ).astype(BF)
        for i in range(2)
    ]
    keep = jnp.where(first, picked[0], picked[1])
    give = jnp.where(first, picked[1], picked[0])
    got = lax.ppermute(give, "c", swap)
    by_shift = [jnp.where(first, keep, got), jnp.where(first, got, keep)]

    spread = [dot(interior_inverse[j, 0], couple).astype(BF) for j in range(2)]
    total = jnp.zeros((1024, 384), F32)
    for j in range(2):
        interior_sol = eliminated[j].astype(F32) - dot(spread[j], by_shift[j])
        total = total + weights[j] * interior_sol
    pieces = lax.all_to_all(total.astype(BF).reshape(8, 128, 384), SHIFT, 0, 0, tiled=True)
    return jnp.sum(pieces.astype(F32), axis=0)[:, None, :]


def solution(mesh):
    fine = Mesh(mesh.devices.reshape(2, 4, 2, 8, 2), ("yl", "x", "yh", "z", "c"))
    in_specs = (
        P(SUB, None, None),
        P(),
        P(SHIFT, SUB, None, None),
        P(SUB, None, None),
        P(SHIFT, SUB, None),
        P(SHIFT),
        P(),
        P(),
    )
    out_specs = P(SHIFT, SUB, None)
    return jax.shard_map(
        on_device, mesh=fine, in_specs=in_specs, out_specs=out_specs, check_vma=False
    )
```

```python
import jax
import jax.numpy as jnp
from jax import lax
from jax.sharding import Mesh, PartitionSpec as P

BF = jnp.bfloat16
F32 = jnp.float32
SUB = ("yh", "z", "c")
EXCHANGE = ("yh", "c", "z")
SHIFT = ("yl", "x")
HALF = 192


def dot(a, b):
    return jnp.dot(a, b, preferred_element_type=F32)


def dot_t(a, b):
    return lax.dot_general(a, b, (((0,), (0,)), ((), ())), preferred_element_type=F32)


def roll(a):
    return jnp.concatenate([a[:, HALF:], a[:, :HALF]], axis=1)


def on_device(
    interior_rhs,
    interface_rhs,
    interior_inverse,
    coupling,
    schur_inverse,
    weights,
    owner_sub,
    index_blocks,
):
    y, z, c = lax.axis_index("yh"), lax.axis_index("z"), lax.axis_index("c")
    swap = [(0, 1), (1, 0)]
    rhs = interior_rhs[0]
    couple = coupling[0]

    def low(shape):
        return lax.broadcasted_iota(jnp.int32, shape, len(shape) - 1) < HALF

    mine = c == 0
    schur_keep = jnp.where(mine, schur_inverse[0], schur_inverse[1])
    schur_give = jnp.where(mine, schur_inverse[1], schur_inverse[0])
    schur_got = lax.ppermute(schur_give, "c", swap)
    schur_own = jnp.concatenate(
        [jnp.where(mine, schur_keep, schur_got), jnp.where(mine, schur_got, schur_keep)], axis=0
    )
    schur_other = lax.ppermute(schur_own, "yh", swap)

    eliminated = [dot(interior_inverse[j, 0], rhs).astype(BF) for j in range(2)]
    coupled = [dot_t(couple, e).astype(BF) for e in eliminated]

    owner = lax.dynamic_index_in_dim(owner_sub, (y * 8 + z) * 2 + c, 0, keepdims=False)
    idx = lax.dynamic_index_in_dim(index_blocks, owner, 0, keepdims=False)
    here, other = idx[:, None], idx[None, :]
    rank = jnp.sum(((here // 64 == other // 64) & (other < here)).astype(jnp.int32), axis=1)
    slot = ((idx // 128) % 8) * 32 + ((idx // 64) % 2) * 16 + rank
    line = lax.broadcasted_iota(jnp.int32, (256, 256), 0)
    hit = line == slot[None, :]
    upper = (idx >= 1024)[None, :]
    pack = jnp.concatenate([(hit & ~upper).astype(BF), (hit & upper).astype(BF)], axis=1)

    low_k = low((256, 384))
    zero = jnp.zeros((), BF)
    packed = []
    rolled = [roll(x) for x in coupled]
    for h in range(2):
        for j in range(2):
            a, b = (coupled[j], rolled[j]) if h == 0 else (rolled[j], coupled[j])
            both = jnp.concatenate([jnp.where(low_k, a, zero), jnp.where(low_k, zero, b)], axis=0)
            packed.append(dot(pack, both).astype(BF).reshape(8, 32, 384))
    packed = jnp.concatenate(packed, axis=0)
    arrived = lax.all_to_all(packed, EXCHANGE, 0, 0, tiled=True).reshape(1024, 384)

    owners = owner_sub.reshape(2, 8, 2).transpose(0, 2, 1).reshape(32)
    names = lax.broadcasted_iota(jnp.int32, (32, 32, 1), 1)
    idx_all = jnp.sum(jnp.where(owners[:, None, None] == names, index_blocks[None], 0), axis=1)
    rows = lax.broadcasted_iota(jnp.int32, (1, 1, 256), 2)
    rows = (rows // 128) * 1024 + z * 128 + rows % 128
    held = jnp.any(idx_all[:, :, None] == rows, axis=1)
    first = lax.broadcasted_iota(jnp.int32, (256, 256), 0)
    second = lax.broadcasted_iota(jnp.int32, (256, 256), 1)
    before = ((first < second) & (first // 64 == second // 64)).astype(BF)
    place = dot(held.astype(BF), before).astype(jnp.int32)
    place = place + 16 * ((lax.broadcasted_iota(jnp.int32, (32, 256), 1) // 64) % 2)
    place = jnp.where(held, place, -1)
    select = (
        (place[:, None, :] == lax.broadcasted_iota(jnp.int32, (32, 32, 256), 1))
        .astype(BF)
        .reshape(1024, 256)
    )

    base = [lax.dynamic_slice_in_dim(interface_rhs, q * 1024 + z * 128, 128, 0) for q in range(2)]
    low_i = low((128, 384))
    plane_rhs = jnp.where(
        y == 0,
        jnp.where(low_i, base[0], roll(base[1])),
        jnp.where(low_i, roll(base[0]), base[1]),
    )

    spread = jnp.concatenate(
        [(weights[j] * dot(interior_inverse[j, 0], couple)).astype(BF) for j in range(2)], axis=1
    )
    direct = weights[0] * eliminated[0].astype(F32) + weights[1] * eliminated[1].astype(F32)

    rows0 = jnp.where(y == 0, schur_own, schur_other)
    rows1 = jnp.where(y == 0, schur_other, schur_own)
    order = (0, -1, 1, -2, 2, -3, 3, 4)
    blocks = []
    for s in order:
        at = (z + s + 8) % 8 * 128
        blocks.append(
            jnp.concatenate(
                [
                    lax.dynamic_slice_in_dim(r, q * 1024 + at, 128, 1)
                    for r in (rows0, rows1)
                    for q in range(2)
                ],
                axis=0,
            )
        )
    schur = jnp.concatenate(blocks, axis=1)
    arrived, select, spread, direct, plane_rhs, schur = lax.optimization_barrier(
        (arrived, select, spread, direct, plane_rhs, schur)
    )

    summed = dot_t(select, arrived)
    summed = jnp.where(low_i, summed[:128], summed[128:])
    reduced = (plane_rhs.astype(F32) - summed).astype(BF)

    up = [(i, (i + 1) % 8) for i in range(8)]
    down = [(i, (i + 7) % 8) for i in range(8)]
    ring = [reduced]
    a = b = reduced
    for s in range(3):
        a = lax.ppermute(a, "z", up)
        b = lax.ppermute(b, "z", down)
        ring += [a, b]
    ring.append(lax.ppermute(a, "z", up))
    solved = dot(schur, jnp.concatenate(ring, axis=0))
    s00, s01, s10, s11 = [solved[128 * i : 128 * (i + 1)] for i in range(4)]
    solved = (jnp.where(low_i, s00, s11) + roll(jnp.where(low_i, s10, s01))).astype(BF)
    both = jnp.concatenate(
        [jnp.where(low_i, solved, zero), jnp.where(low_i, zero, solved)], axis=0
    )
    answers = dot(select, both).astype(BF).reshape(32, 32, 384)
    back = lax.all_to_all(answers, EXCHANGE, 0, 0, tiled=True).reshape(4, 256, 384)
    picked = []
    for j in range(2):
        from0, from1 = dot_t(pack, back[j]), dot_t(pack, back[2 + j])
        straight = jnp.where(low_k, from0[:256], from1[256:])
        crossed = jnp.where(low_k, from1[:256], from0[256:])
        picked.append((straight + roll(crossed)).astype(BF))
    total = direct - dot(spread, jnp.concatenate(picked, axis=0))
    pieces = lax.all_to_all(total.astype(BF).reshape(8, 128, 384), SHIFT, 0, 0, tiled=True)
    return jnp.sum(pieces.reshape(8, 128, 1, 384).astype(F32), axis=0)


def solution(mesh):
    fine = Mesh(mesh.devices.reshape(2, 4, 2, 8, 2), ("yl", "x", "yh", "z", "c"))
    in_specs = (
        P(SUB, None, None),
        P(),
        P(SHIFT, SUB, None, None),
        P(SUB, None, None),
        P(SHIFT, SUB, None),
        P(SHIFT),
        P(),
        P(),
    )
    out_specs = P(SHIFT, SUB, None)
    return jax.shard_map(
        on_device, mesh=fine, in_specs=in_specs, out_specs=out_specs, check_vma=False
    )
```

```python
import jax
import jax.numpy as jnp
from jax import lax
from jax.experimental import pallas as pl
from jax.experimental.pallas import tpu as pltpu
from jax.sharding import Mesh, PartitionSpec as P

BF = jnp.bfloat16
F32 = jnp.float32
SUB = ("yh", "z", "c")
EXCHANGE = ("yh", "c", "z")
SHIFT = ("yl", "x")
HALF = 192


def dot(a, b):
    return jnp.dot(a, b, preferred_element_type=F32)


def dot_t(a, b):
    return lax.dot_general(a, b, (((0,), (0,)), ((), ())), preferred_element_type=F32)


def roll(a):
    return jnp.concatenate([a[:, HALF:], a[:, :HALF]], axis=1)


def roll32(a):
    return pltpu.roll(a, HALF, 1)


def start_kernel(
    position_ref,
    owner_ref,
    blocks_ref,
    inverse_ref,
    rhs_ref,
    couple_ref,
    eliminated_ref,
    packed_ref,
    pack_ref,
    pick_ref,
    total_ref,
):
    j, i = pl.program_id(0), pl.program_id(1)

    @pl.when((j == 0) & (i == 0))
    def _():
        row = blocks_ref[pl.ds(owner_ref[position_ref[0]], 1), :]
        across = jnp.broadcast_to(row, (256, 256))
        down = jnp.broadcast_to(row.astype(F32), (256, 256)).T.astype(jnp.int32)
        same = (across >> 6) == (down >> 6)
        rank = jnp.sum((same & (down < across)).astype(F32), axis=0, keepdims=True)
        slot = ((row >> 7) & 7) * 32 + ((row >> 6) & 1) * 16 + rank.astype(jnp.int32)
        hit = lax.broadcasted_iota(jnp.int32, (256, 256), 0) == slot
        pack_ref[:, :256] = jnp.where(hit & (across < 1024), 1.0, 0.0).astype(BF)
        pack_ref[:, 256:] = jnp.where(hit & (across >= 1024), 1.0, 0.0).astype(BF)
        rank = jnp.sum((same & (across < down)).astype(F32), axis=1, keepdims=True)
        slot = ((down >> 7) & 7) * 32 + ((down >> 6) & 1) * 16 + rank.astype(jnp.int32)
        hit = lax.broadcasted_iota(jnp.int32, (256, 256), 1) == slot
        pick_ref[:256] = jnp.where(hit & (down < 1024), 1.0, 0.0).astype(BF)
        pick_ref[256:] = jnp.where(hit & (down >= 1024), 1.0, 0.0).astype(BF)

    @pl.when(i == 0)
    def _():
        total_ref[...] = jnp.zeros_like(total_ref)

    part = dot(inverse_ref[0, 0], rhs_ref[0]).astype(BF)
    eliminated_ref[0] = part
    total_ref[...] += dot_t(couple_ref[0], part)

    @pl.when(i == pl.num_programs(1) - 1)
    def _():
        coupled = total_ref[...].astype(BF).astype(F32)
        turned = roll32(coupled)
        low = lax.broadcasted_iota(jnp.int32, (256, 384), 1) < HALF
        for h, (a, b) in enumerate(((coupled, turned), (turned, coupled))):
            a = jnp.where(low, a, 0.0).astype(BF)
            b = jnp.where(low, 0.0, b).astype(BF)
            packed_ref[h, 0] = (dot(pack_ref[:, :256], a) + dot(pack_ref[:, 256:], b)).astype(BF)


def start(position, owner_sub, index_blocks, inverse, rhs, couple, rows=1024):
    steps = 1024 // rows
    smem = pl.BlockSpec(memory_space=pltpu.SMEM)
    return pl.pallas_call(
        start_kernel,
        grid=(2, steps),
        in_specs=[
            smem,
            smem,
            pl.BlockSpec((32, 256), lambda j, i: (0, 0)),
            pl.BlockSpec((1, 1, rows, 1024), lambda j, i: (j, 0, i, 0)),
            pl.BlockSpec((1, 1024, 384), lambda j, i: (0, 0, 0)),
            pl.BlockSpec((1, rows, 256), lambda j, i: (0, i, 0)),
        ],
        out_specs=[
            pl.BlockSpec((1, rows, 384), lambda j, i: (j, i, 0)),
            pl.BlockSpec((2, 1, 256, 384), lambda j, i: (0, j, 0, 0)),
            pl.BlockSpec((256, 512), lambda j, i: (0, 0)),
            pl.BlockSpec((512, 256), lambda j, i: (0, 0)),
        ],
        out_shape=[
            jax.ShapeDtypeStruct((2, 1024, 384), BF),
            jax.ShapeDtypeStruct((2, 2, 256, 384), BF),
            jax.ShapeDtypeStruct((256, 512), BF),
            jax.ShapeDtypeStruct((512, 256), BF),
        ],
        scratch_shapes=[pltpu.VMEM((256, 384), F32)],
        name="start",
    )(position, owner_sub, index_blocks, inverse, rhs, couple)


def finish_kernel(
    weights_ref, back_ref, pick_ref, spread0_ref, spread1_ref, eliminated_ref, out_ref, picked_ref
):
    @pl.when(pl.program_id(0) == 0)
    def _():
        low = lax.broadcasted_iota(jnp.int32, (256, 384), 1) < HALF
        for j in range(2):
            top = [dot(pick_ref[:256], back_ref[2 * h + j]) for h in range(2)]
            end = [dot(pick_ref[256:], back_ref[2 * h + j]) for h in range(2)]
            straight = jnp.where(low, top[0], end[1])
            crossed = jnp.where(low, top[1], end[0])
            picked_ref[j] = (straight + roll32(crossed)).astype(BF)

    total = weights_ref[0] * eliminated_ref[0].astype(F32)
    total += weights_ref[1] * eliminated_ref[1].astype(F32)
    total -= dot(spread0_ref[...], picked_ref[0]) + dot(spread1_ref[...], picked_ref[1])
    out_ref[...] = total.astype(BF)


def finish(weights, back, pick, spread0, spread1, eliminated, rows=512):
    return pl.pallas_call(
        finish_kernel,
        grid=(1024 // rows,),
        in_specs=[
            pl.BlockSpec(memory_space=pltpu.SMEM),
            pl.BlockSpec((4, 256, 384), lambda i: (0, 0, 0)),
            pl.BlockSpec((512, 256), lambda i: (0, 0)),
            pl.BlockSpec((rows, 256), lambda i: (i, 0)),
            pl.BlockSpec((rows, 256), lambda i: (i, 0)),
            pl.BlockSpec((2, rows, 384), lambda i: (0, i, 0)),
        ],
        out_specs=pl.BlockSpec((rows, 384), lambda i: (i, 0)),
        out_shape=jax.ShapeDtypeStruct((1024, 384), BF),
        scratch_shapes=[pltpu.VMEM((2, 256, 384), BF)],
        name="finish",
    )(weights, back, pick, spread0, spread1, eliminated)


def on_device(
    interior_rhs,
    interface_rhs,
    interior_inverse,
    coupling,
    schur_inverse,
    weights,
    owner_sub,
    index_blocks,
):
    y, z, c = lax.axis_index("yh"), lax.axis_index("z"), lax.axis_index("c")
    swap = [(0, 1), (1, 0)]

    def low(shape):
        return lax.broadcasted_iota(jnp.int32, shape, len(shape) - 1) < HALF

    position = ((y * 8 + z) * 2 + c).astype(jnp.int32)
    eliminated, packed, _, pick = start(
        position[None], owner_sub, index_blocks, interior_inverse, interior_rhs, coupling
    )
    zero = jnp.zeros((), BF)
    packed, schur_inverse = lax.optimization_barrier((packed, schur_inverse))
    packed = packed.reshape(32, 32, 384)
    arrived = lax.all_to_all(packed, EXCHANGE, 0, 0, tiled=True).reshape(1024, 384)

    keep = lax.dynamic_index_in_dim(schur_inverse, c, 0, keepdims=False)
    give = lax.dynamic_index_in_dim(schur_inverse, 1 - c, 0, keepdims=False)
    across = lax.ppermute(give, ("yh", "c"), [(0, 3), (1, 2), (2, 1), (3, 0)])
    beyond = lax.ppermute(keep, "yh", swap)
    beside = lax.ppermute(give, "c", swap)

    owners = owner_sub.reshape(2, 8, 2).transpose(0, 2, 1).reshape(32)
    names = lax.broadcasted_iota(jnp.int32, (32, 32, 1), 1)
    idx_all = jnp.sum(jnp.where(owners[:, None, None] == names, index_blocks[None], 0), axis=1)
    rows = lax.broadcasted_iota(jnp.int32, (1, 1, 256), 2)
    rows = (rows // 128) * 1024 + z * 128 + rows % 128
    held = jnp.any(idx_all[:, :, None] == rows, axis=1)
    first = lax.broadcasted_iota(jnp.int32, (256, 256), 0)
    second = lax.broadcasted_iota(jnp.int32, (256, 256), 1)
    before = ((first < second) & (first // 64 == second // 64)).astype(BF)
    place = dot(held.astype(BF), before).astype(jnp.int32)
    place = place + 16 * ((lax.broadcasted_iota(jnp.int32, (32, 256), 1) // 64) % 2)
    place = jnp.where(held, place, -1)
    select = (
        (place[:, None, :] == lax.broadcasted_iota(jnp.int32, (32, 32, 256), 1))
        .astype(BF)
        .reshape(1024, 256)
    )

    base = [lax.dynamic_slice_in_dim(interface_rhs, q * 1024 + z * 128, 128, 0) for q in range(2)]
    low_i = low((128, 384))
    plane_rhs = jnp.where(
        y == 0,
        jnp.where(low_i, base[0], roll(base[1])),
        jnp.where(low_i, roll(base[0]), base[1]),
    )

    spread = [(weights[j] * dot(interior_inverse[j, 0], coupling[0])).astype(BF) for j in range(2)]

    schur = jnp.concatenate([keep, beside, beyond, across], axis=0)
    arrived, select, spread, plane_rhs, schur = lax.optimization_barrier(
        (arrived, select, spread, plane_rhs, schur)
    )

    summed = dot_t(select, arrived)
    summed = jnp.where(low_i, summed[:128], summed[128:])
    reduced = (plane_rhs.astype(F32) - summed).astype(BF)

    up = [(i, (i + 1) % 8) for i in range(8)]
    down = [(i, (i + 7) % 8) for i in range(8)]
    gathered = jnp.zeros((1024, 384), BF)

    def put(block, step):
        return lax.dynamic_update_slice(gathered, block, (((z + step) & 7) * 128, 0))

    gathered = put(reduced, 0)
    a = b = reduced
    for s in range(1, 4):
        a = lax.ppermute(a, "z", up)
        b = lax.ppermute(b, "z", down)
        gathered = put(a, -s)
        gathered = put(b, s)
    gathered = put(lax.ppermute(a, "z", up), 4)
    from0, from1 = dot(schur[:, :1024], gathered), dot(schur[:, 1024:], gathered)

    def half(x, q):
        x = jnp.where(y == q, x[:128], x[128:])
        return jnp.where(c == 0, x, jnp.concatenate([x[64:], x[:64]], axis=0))

    straight = jnp.where(low_i, half(from0, 0), half(from1, 1))
    crossed = jnp.where(low_i, half(from0, 1), half(from1, 0))
    solved = (straight + roll(crossed)).astype(BF)
    both = jnp.concatenate(
        [jnp.where(low_i, solved, zero), jnp.where(low_i, zero, solved)], axis=0
    )
    answers = dot(select, both).astype(BF).reshape(32, 32, 384)
    back = lax.all_to_all(answers, EXCHANGE, 0, 0, tiled=True).reshape(4, 256, 384)
    total = finish(weights, back, pick, *spread, eliminated)
    pieces = lax.all_to_all(total.reshape(8, 128, 384), SHIFT, 0, 0, tiled=True)
    return jnp.sum(pieces.reshape(8, 128, 1, 384).astype(F32), axis=0)


def solution(mesh):
    fine = Mesh(mesh.devices.reshape(2, 4, 2, 8, 2), ("yl", "x", "yh", "z", "c"))
    in_specs = (
        P(SUB, None, None),
        P(),
        P(SHIFT, SUB, None, None),
        P(SUB, None, None),
        P(SHIFT, SUB, None),
        P(SHIFT),
        P(),
        P(),
    )
    out_specs = P(SHIFT, SUB, None)
    return jax.shard_map(
        on_device, mesh=fine, in_specs=in_specs, out_specs=out_specs, check_vma=False
    )
```

```python
import jax
import jax.numpy as jnp
from jax import lax
from jax.experimental import pallas as pl
from jax.experimental.pallas import tpu as pltpu
from jax.sharding import Mesh, PartitionSpec as P

BF = jnp.bfloat16
F32 = jnp.float32
SUB = ("yh", "z", "c")
EXCHANGE = ("yh", "c", "z")
SHIFT = ("yl", "x")
HALF = 192


def dot(a, b):
    return jnp.dot(a, b, preferred_element_type=F32)


def dot_t(a, b):
    return lax.dot_general(a, b, (((0,), (0,)), ((), ())), preferred_element_type=F32)


def roll(a):
    return jnp.concatenate([a[:, HALF:], a[:, :HALF]], axis=1)


def roll32(a):
    return pltpu.roll(a, HALF, 1)


def start_kernel(
    position_ref,
    owner_ref,
    blocks_ref,
    inverse_ref,
    rhs_ref,
    couple_ref,
    eliminated_ref,
    packed_ref,
    pack_ref,
    pick_ref,
    total_ref,
):
    j, i = pl.program_id(0), pl.program_id(1)

    @pl.when((j == 0) & (i == 0))
    def _():
        row = blocks_ref[pl.ds(owner_ref[position_ref[0]], 1), :]
        across = jnp.broadcast_to(row, (256, 256))
        down = jnp.broadcast_to(row.astype(F32), (256, 256)).T.astype(jnp.int32)
        same = (across >> 6) == (down >> 6)
        rank = jnp.sum((same & (down < across)).astype(F32), axis=0, keepdims=True)
        slot = ((row >> 7) & 7) * 32 + ((row >> 6) & 1) * 16 + rank.astype(jnp.int32)
        hit = lax.broadcasted_iota(jnp.int32, (256, 256), 0) == slot
        pack_ref[:, :256] = jnp.where(hit & (across < 1024), 1.0, 0.0).astype(BF)
        pack_ref[:, 256:] = jnp.where(hit & (across >= 1024), 1.0, 0.0).astype(BF)
        rank = jnp.sum((same & (across < down)).astype(F32), axis=1, keepdims=True)
        slot = ((down >> 7) & 7) * 32 + ((down >> 6) & 1) * 16 + rank.astype(jnp.int32)
        hit = lax.broadcasted_iota(jnp.int32, (256, 256), 1) == slot
        pick_ref[:256] = jnp.where(hit & (down < 1024), 1.0, 0.0).astype(BF)
        pick_ref[256:] = jnp.where(hit & (down >= 1024), 1.0, 0.0).astype(BF)

    @pl.when(i == 0)
    def _():
        total_ref[...] = jnp.zeros_like(total_ref)

    part = dot(inverse_ref[0, 0], rhs_ref[0]).astype(BF)
    eliminated_ref[0] = part
    total_ref[...] += dot_t(couple_ref[0], part)

    @pl.when(i == pl.num_programs(1) - 1)
    def _():
        coupled = total_ref[...].astype(BF).astype(F32)
        turned = roll32(coupled)
        low = lax.broadcasted_iota(jnp.int32, (256, 384), 1) < HALF
        for h, (a, b) in enumerate(((coupled, turned), (turned, coupled))):
            a = jnp.where(low, a, 0.0).astype(BF)
            b = jnp.where(low, 0.0, b).astype(BF)
            packed_ref[h, 0] = (dot(pack_ref[:, :256], a) + dot(pack_ref[:, 256:], b)).astype(BF)


def start(position, owner_sub, index_blocks, inverse, rhs, couple, rows=1024):
    steps = 1024 // rows
    smem = pl.BlockSpec(memory_space=pltpu.SMEM)
    return pl.pallas_call(
        start_kernel,
        grid=(2, steps),
        in_specs=[
            smem,
            smem,
            pl.BlockSpec((32, 256), lambda j, i: (0, 0)),
            pl.BlockSpec((1, 1, rows, 1024), lambda j, i: (j, 0, i, 0)),
            pl.BlockSpec((1, 1024, 384), lambda j, i: (0, 0, 0)),
            pl.BlockSpec((1, rows, 256), lambda j, i: (0, i, 0)),
        ],
        out_specs=[
            pl.BlockSpec((1, rows, 384), lambda j, i: (j, i, 0)),
            pl.BlockSpec((2, 1, 256, 384), lambda j, i: (0, j, 0, 0)),
            pl.BlockSpec((256, 512), lambda j, i: (0, 0)),
            pl.BlockSpec((512, 256), lambda j, i: (0, 0)),
        ],
        out_shape=[
            jax.ShapeDtypeStruct((2, 1024, 384), BF),
            jax.ShapeDtypeStruct((2, 2, 256, 384), BF),
            jax.ShapeDtypeStruct((256, 512), BF),
            jax.ShapeDtypeStruct((512, 256), BF),
        ],
        scratch_shapes=[pltpu.VMEM((256, 384), F32)],
        name="start",
    )(position, owner_sub, index_blocks, inverse, rhs, couple)


def finish_kernel(
    weights_ref, back_ref, pick_ref, spread0_ref, spread1_ref, eliminated_ref, out_ref, picked_ref
):
    @pl.when(pl.program_id(0) == 0)
    def _():
        low = lax.broadcasted_iota(jnp.int32, (256, 384), 1) < HALF
        for j in range(2):
            top = [dot(pick_ref[:256], back_ref[2 * h + j]) for h in range(2)]
            end = [dot(pick_ref[256:], back_ref[2 * h + j]) for h in range(2)]
            straight = jnp.where(low, top[0], end[1])
            crossed = jnp.where(low, top[1], end[0])
            picked_ref[j] = (straight + roll32(crossed)).astype(BF)

    total = weights_ref[0] * eliminated_ref[0].astype(F32)
    total += weights_ref[1] * eliminated_ref[1].astype(F32)
    total -= dot(spread0_ref[...], picked_ref[0]) + dot(spread1_ref[...], picked_ref[1])
    out_ref[...] = total.astype(BF)


def finish(weights, back, pick, spread0, spread1, eliminated, rows=512):
    return pl.pallas_call(
        finish_kernel,
        grid=(1024 // rows,),
        in_specs=[
            pl.BlockSpec(memory_space=pltpu.SMEM),
            pl.BlockSpec((4, 256, 384), lambda i: (0, 0, 0)),
            pl.BlockSpec((512, 256), lambda i: (0, 0)),
            pl.BlockSpec((rows, 256), lambda i: (i, 0)),
            pl.BlockSpec((rows, 256), lambda i: (i, 0)),
            pl.BlockSpec((2, rows, 384), lambda i: (0, i, 0)),
        ],
        out_specs=pl.BlockSpec((rows, 384), lambda i: (i, 0)),
        out_shape=jax.ShapeDtypeStruct((1024, 384), BF),
        scratch_shapes=[pltpu.VMEM((2, 256, 384), BF)],
        name="finish",
    )(weights, back, pick, spread0, spread1, eliminated)


def on_device(
    interior_rhs,
    interface_rhs,
    interior_inverse,
    coupling,
    schur_inverse,
    weights,
    owner_sub,
    index_blocks,
):
    y, z, c = lax.axis_index("yh"), lax.axis_index("z"), lax.axis_index("c")
    swap = [(0, 1), (1, 0)]

    def low(shape):
        return lax.broadcasted_iota(jnp.int32, shape, len(shape) - 1) < HALF

    position = ((y * 8 + z) * 2 + c).astype(jnp.int32)
    eliminated, packed, _, pick = start(
        position[None], owner_sub, index_blocks, interior_inverse, interior_rhs, coupling
    )
    zero = jnp.zeros((), BF)
    packed, schur_inverse = lax.optimization_barrier((packed, schur_inverse))
    packed = packed.reshape(32, 32, 384)
    arrived = lax.all_to_all(packed, EXCHANGE, 0, 0, tiled=True).reshape(1024, 384)

    keep = lax.dynamic_index_in_dim(schur_inverse, c, 0, keepdims=False)
    give = lax.dynamic_index_in_dim(schur_inverse, 1 - c, 0, keepdims=False)
    across = lax.ppermute(give, ("yh", "c"), [(0, 3), (1, 2), (2, 1), (3, 0)])
    beyond = lax.ppermute(keep, "yh", swap)
    beside = lax.ppermute(give, "c", swap)

    owners = owner_sub.reshape(2, 8, 2).transpose(0, 2, 1).reshape(32)
    names = lax.broadcasted_iota(jnp.int32, (32, 32, 1), 1)
    idx_all = jnp.sum(jnp.where(owners[:, None, None] == names, index_blocks[None], 0), axis=1)
    rows = lax.broadcasted_iota(jnp.int32, (1, 1, 256), 2)
    rows = (rows // 128) * 1024 + z * 128 + rows % 128
    held = jnp.any(idx_all[:, :, None] == rows, axis=1)
    first = lax.broadcasted_iota(jnp.int32, (256, 256), 0)
    second = lax.broadcasted_iota(jnp.int32, (256, 256), 1)
    before = ((first < second) & (first // 64 == second // 64)).astype(BF)
    place = dot(held.astype(BF), before).astype(jnp.int32)
    place = place + 16 * ((lax.broadcasted_iota(jnp.int32, (32, 256), 1) // 64) % 2)
    place = jnp.where(held, place, -1)
    select = (
        (place[:, None, :] == lax.broadcasted_iota(jnp.int32, (32, 32, 256), 1))
        .astype(BF)
        .reshape(1024, 256)
    )

    base = [lax.dynamic_slice_in_dim(interface_rhs, q * 1024 + z * 128, 128, 0) for q in range(2)]
    low_i = low((128, 384))
    plane_rhs = jnp.where(
        y == 0,
        jnp.where(low_i, base[0], roll(base[1])),
        jnp.where(low_i, roll(base[0]), base[1]),
    )

    spread = [(weights[j] * dot(interior_inverse[j, 0], coupling[0])).astype(BF) for j in range(2)]

    arrived, select, spread, plane_rhs = lax.optimization_barrier(
        (arrived, select, spread, plane_rhs)
    )

    summed = dot_t(select, arrived)
    summed = jnp.where(low_i, summed[:128], summed[128:])
    reduced = (plane_rhs.astype(F32) - summed).astype(BF)

    up = [(i, (i + 1) % 8) for i in range(8)]
    down = [(i, (i + 7) % 8) for i in range(8)]
    gathered = jnp.zeros((1024, 384), BF)

    def put(block, step):
        return lax.dynamic_update_slice(gathered, block, (((z + step) & 7) * 128, 0))

    up2 = [(i, (i + 2) % 8) for i in range(8)]
    down2 = [(i, (i + 6) % 8) for i in range(8)]
    below1, above1 = lax.ppermute(reduced, "z", up), lax.ppermute(reduced, "z", down)
    below2, above2 = lax.ppermute(reduced, "z", up2), lax.ppermute(reduced, "z", down2)
    below1, keep, beside, beyond, across = lax.optimization_barrier(
        (below1, keep, beside, beyond, across)
    )
    schur = jnp.concatenate([keep, beside, beyond, across], axis=0)
    below1, keep, beside, beyond, across = lax.optimization_barrier(
        (below1, keep, beside, beyond, across)
    )
    schur = jnp.concatenate([keep, beside, beyond, across], axis=0)
    below3, above3 = lax.ppermute(below2, "z", up), lax.ppermute(above2, "z", down)
    opposite = lax.ppermute(below2, "z", up2)
    for step, block in (
        (0, reduced),
        (-1, below1),
        (1, above1),
        (-2, below2),
        (2, above2),
        (-3, below3),
        (3, above3),
        (4, opposite),
    ):
        gathered = put(block, step)
    from0, from1 = dot(schur[:, :1024], gathered), dot(schur[:, 1024:], gathered)

    def half(x, q):
        x = jnp.where(y == q, x[:128], x[128:])
        return jnp.where(c == 0, x, jnp.concatenate([x[64:], x[:64]], axis=0))

    straight = jnp.where(low_i, half(from0, 0), half(from1, 1))
    crossed = jnp.where(low_i, half(from0, 1), half(from1, 0))
    solved = (straight + roll(crossed)).astype(BF)
    both = jnp.concatenate(
        [jnp.where(low_i, solved, zero), jnp.where(low_i, zero, solved)], axis=0
    )
    answers = dot(select, both).astype(BF).reshape(32, 32, 384)
    back = lax.all_to_all(answers, EXCHANGE, 0, 0, tiled=True).reshape(4, 256, 384)
    total = finish(weights, back, pick, *spread, eliminated)
    pieces = lax.all_to_all(total.reshape(8, 128, 384), SHIFT, 0, 0, tiled=True)
    return jnp.sum(pieces.reshape(8, 128, 1, 384).astype(F32), axis=0)


def solution(mesh):
    fine = Mesh(mesh.devices.reshape(2, 4, 2, 8, 2), ("yl", "x", "yh", "z", "c"))
    in_specs = (
        P(SUB, None, None),
        P(),
        P(SHIFT, SUB, None, None),
        P(SUB, None, None),
        P(SHIFT, SUB, None),
        P(SHIFT),
        P(),
        P(),
    )
    out_specs = P(SHIFT, SUB, None)

    return jax.shard_map(
        on_device, mesh=fine, in_specs=in_specs, out_specs=out_specs, check_vma=False
    )
```

```python
import jax
import jax.numpy as jnp
from jax import lax
from jax.experimental import pallas as pl
from jax.experimental.pallas import tpu as pltpu
from jax.sharding import Mesh, PartitionSpec as P

BF = jnp.bfloat16
F32 = jnp.float32
SUB = ("yh", "z", "c")
EXCHANGE = ("yh", "c", "z")
SHIFT = ("yl", "x")
HALF = 192


def dot(a, b):
    return jnp.dot(a, b, preferred_element_type=F32)


def dot_t(a, b):
    return lax.dot_general(a, b, (((0,), (0,)), ((), ())), preferred_element_type=F32)


def roll(a):
    return jnp.concatenate([a[:, HALF:], a[:, :HALF]], axis=1)


def roll32(a):
    return pltpu.roll(a, HALF, 1)


def start_kernel(
    position_ref,
    owner_ref,
    blocks_ref,
    inverse_ref,
    rhs_ref,
    couple_ref,
    eliminated_ref,
    packed_ref,
    pack_ref,
    pick_ref,
    total_ref,
):
    j, i = pl.program_id(0), pl.program_id(1)

    @pl.when((j == 0) & (i == 0))
    def _():
        row = blocks_ref[pl.ds(owner_ref[position_ref[0]], 1), :]
        across = jnp.broadcast_to(row, (256, 256))
        down = jnp.broadcast_to(row.astype(F32), (256, 256)).T.astype(jnp.int32)
        same = (across >> 6) == (down >> 6)
        rank = jnp.sum((same & (down < across)).astype(F32), axis=0, keepdims=True)
        slot = ((row >> 7) & 7) * 32 + ((row >> 6) & 1) * 16 + rank.astype(jnp.int32)
        hit = lax.broadcasted_iota(jnp.int32, (256, 256), 0) == slot
        pack_ref[:, :256] = jnp.where(hit & (across < 1024), 1.0, 0.0).astype(BF)
        pack_ref[:, 256:] = jnp.where(hit & (across >= 1024), 1.0, 0.0).astype(BF)
        rank = jnp.sum((same & (across < down)).astype(F32), axis=1, keepdims=True)
        slot = ((down >> 7) & 7) * 32 + ((down >> 6) & 1) * 16 + rank.astype(jnp.int32)
        hit = lax.broadcasted_iota(jnp.int32, (256, 256), 1) == slot
        pick_ref[:256] = jnp.where(hit & (down < 1024), 1.0, 0.0).astype(BF)
        pick_ref[256:] = jnp.where(hit & (down >= 1024), 1.0, 0.0).astype(BF)

    @pl.when(i == 0)
    def _():
        total_ref[...] = jnp.zeros_like(total_ref)

    part = dot(inverse_ref[0, 0], rhs_ref[0]).astype(BF)
    eliminated_ref[0] = part
    total_ref[...] += dot_t(couple_ref[0], part)

    @pl.when(i == pl.num_programs(1) - 1)
    def _():
        coupled = total_ref[...].astype(BF).astype(F32)
        turned = roll32(coupled)
        low = lax.broadcasted_iota(jnp.int32, (256, 384), 1) < HALF
        for h, (a, b) in enumerate(((coupled, turned), (turned, coupled))):
            a = jnp.where(low, a, 0.0).astype(BF)
            b = jnp.where(low, 0.0, b).astype(BF)
            packed_ref[h, 0] = (dot(pack_ref[:, :256], a) + dot(pack_ref[:, 256:], b)).astype(BF)


def start(position, owner_sub, index_blocks, inverse, rhs, couple, rows=1024):
    steps = 1024 // rows
    smem = pl.BlockSpec(memory_space=pltpu.SMEM)
    return pl.pallas_call(
        start_kernel,
        grid=(2, steps),
        in_specs=[
            smem,
            smem,
            pl.BlockSpec((32, 256), lambda j, i: (0, 0)),
            pl.BlockSpec((1, 1, rows, 1024), lambda j, i: (j, 0, i, 0)),
            pl.BlockSpec((1, 1024, 384), lambda j, i: (0, 0, 0)),
            pl.BlockSpec((1, rows, 256), lambda j, i: (0, i, 0)),
        ],
        out_specs=[
            pl.BlockSpec((1, rows, 384), lambda j, i: (j, i, 0)),
            pl.BlockSpec((2, 1, 256, 384), lambda j, i: (0, j, 0, 0)),
            pl.BlockSpec((256, 512), lambda j, i: (0, 0)),
            pl.BlockSpec((512, 256), lambda j, i: (0, 0)),
        ],
        out_shape=[
            jax.ShapeDtypeStruct((2, 1024, 384), BF),
            jax.ShapeDtypeStruct((2, 2, 256, 384), BF),
            jax.ShapeDtypeStruct((256, 512), BF),
            jax.ShapeDtypeStruct((512, 256), BF),
        ],
        scratch_shapes=[pltpu.VMEM((256, 384), F32)],
        name="start",
    )(position, owner_sub, index_blocks, inverse, rhs, couple)


def finish_kernel(
    weights_ref, back_ref, pick_ref, spread0_ref, spread1_ref, eliminated_ref, out_ref, picked_ref
):
    @pl.when(pl.program_id(0) == 0)
    def _():
        low = lax.broadcasted_iota(jnp.int32, (256, 384), 1) < HALF
        for j in range(2):
            top = [dot(pick_ref[:256], back_ref[2 * h + j]) for h in range(2)]
            end = [dot(pick_ref[256:], back_ref[2 * h + j]) for h in range(2)]
            straight = jnp.where(low, top[0], end[1])
            crossed = jnp.where(low, top[1], end[0])
            picked_ref[j] = (straight + roll32(crossed)).astype(BF)

    total = weights_ref[0] * eliminated_ref[0].astype(F32)
    total += weights_ref[1] * eliminated_ref[1].astype(F32)
    total -= dot(spread0_ref[...], picked_ref[0]) + dot(spread1_ref[...], picked_ref[1])
    out_ref[...] = total.astype(BF)


def finish(weights, back, pick, spread0, spread1, eliminated, rows=512):
    return pl.pallas_call(
        finish_kernel,
        grid=(1024 // rows,),
        in_specs=[
            pl.BlockSpec(memory_space=pltpu.SMEM),
            pl.BlockSpec((4, 256, 384), lambda i: (0, 0, 0)),
            pl.BlockSpec((512, 256), lambda i: (0, 0)),
            pl.BlockSpec((rows, 256), lambda i: (i, 0)),
            pl.BlockSpec((rows, 256), lambda i: (i, 0)),
            pl.BlockSpec((2, rows, 384), lambda i: (0, i, 0)),
        ],
        out_specs=pl.BlockSpec((rows, 384), lambda i: (i, 0)),
        out_shape=jax.ShapeDtypeStruct((1024, 384), BF),
        scratch_shapes=[pltpu.VMEM((2, 256, 384), BF)],
        name="finish",
    )(weights, back, pick, spread0, spread1, eliminated)


def on_device(
    interior_rhs,
    interface_rhs,
    interior_inverse,
    coupling,
    schur_inverse,
    weights,
    owner_sub,
    index_blocks,
):
    y, z, c = lax.axis_index("yh"), lax.axis_index("z"), lax.axis_index("c")
    swap = [(0, 1), (1, 0)]

    def low(shape):
        return lax.broadcasted_iota(jnp.int32, shape, len(shape) - 1) < HALF

    position = ((y * 8 + z) * 2 + c).astype(jnp.int32)
    eliminated, packed, _, pick = start(
        position[None], owner_sub, index_blocks, interior_inverse, interior_rhs, coupling
    )
    zero = jnp.zeros((), BF)
    packed, schur_inverse = lax.optimization_barrier((packed, schur_inverse))
    packed = packed.reshape(32, 32, 384)
    arrived = lax.all_to_all(packed, EXCHANGE, 0, 0, tiled=True).reshape(1024, 384)

    keep = lax.dynamic_index_in_dim(schur_inverse, c, 0, keepdims=False)
    give = lax.dynamic_index_in_dim(schur_inverse, 1 - c, 0, keepdims=False)
    across = lax.ppermute(give, ("yh", "c"), [(0, 3), (1, 2), (2, 1), (3, 0)])
    beyond = lax.ppermute(keep, "yh", swap)
    beside = lax.ppermute(give, "c", swap)

    owners = owner_sub.reshape(2, 8, 2).transpose(0, 2, 1).reshape(32)
    names = lax.broadcasted_iota(jnp.int32, (32, 32, 1), 1)
    idx_all = jnp.sum(jnp.where(owners[:, None, None] == names, index_blocks[None], 0), axis=1)
    rows = lax.broadcasted_iota(jnp.int32, (1, 1, 256), 2)
    rows = (rows // 128) * 1024 + z * 128 + rows % 128
    held = jnp.any(idx_all[:, :, None] == rows, axis=1)
    first = lax.broadcasted_iota(jnp.int32, (256, 256), 0)
    second = lax.broadcasted_iota(jnp.int32, (256, 256), 1)
    before = ((first < second) & (first // 64 == second // 64)).astype(BF)
    place = dot(held.astype(BF), before).astype(jnp.int32)
    place = place + 16 * ((lax.broadcasted_iota(jnp.int32, (32, 256), 1) // 64) % 2)
    place = jnp.where(held, place, -1)
    select = (
        (place[:, None, :] == lax.broadcasted_iota(jnp.int32, (32, 32, 256), 1))
        .astype(BF)
        .reshape(1024, 256)
    )

    base = [lax.dynamic_slice_in_dim(interface_rhs, q * 1024 + z * 128, 128, 0) for q in range(2)]
    low_i = low((128, 384))
    plane_rhs = jnp.where(
        y == 0,
        jnp.where(low_i, base[0], roll(base[1])),
        jnp.where(low_i, roll(base[0]), base[1]),
    )

    spread = [(weights[j] * dot(interior_inverse[j, 0], coupling[0])).astype(BF) for j in range(2)]

    arrived, select, spread, plane_rhs = lax.optimization_barrier(
        (arrived, select, spread, plane_rhs)
    )

    summed = dot_t(select, arrived)
    summed = jnp.where(low_i, summed[:128], summed[128:])
    reduced = (plane_rhs.astype(F32) - summed).astype(BF)

    up = [(i, (i + 1) % 8) for i in range(8)]
    down = [(i, (i + 7) % 8) for i in range(8)]
    gathered = jnp.zeros((1024, 384), BF)

    def put(block, step):
        return lax.dynamic_update_slice(gathered, block, (((z + step) & 7) * 128, 0))

    up2 = [(i, (i + 2) % 8) for i in range(8)]
    down2 = [(i, (i + 6) % 8) for i in range(8)]
    below2 = lax.ppermute(reduced, "z", up2)
    above2 = lax.ppermute(reduced, "z", down2)
    below1, above1 = lax.ppermute(reduced, "z", up), lax.ppermute(reduced, "z", down)
    below2, keep, beside, beyond, across = lax.optimization_barrier(
        (below2, keep, beside, beyond, across)
    )
    schur = jnp.concatenate([keep, beside, beyond, across], axis=0)
    opposite = lax.ppermute(below2, "z", up2)
    below3, above3 = lax.ppermute(below2, "z", up), lax.ppermute(above2, "z", down)
    for step, block in (
        (0, reduced),
        (-1, below1),
        (1, above1),
        (-2, below2),
        (2, above2),
        (-3, below3),
        (3, above3),
        (4, opposite),
    ):
        gathered = put(block, step)
    from0, from1 = dot(schur[:, :1024], gathered), dot(schur[:, 1024:], gathered)

    def half(x, q):
        x = jnp.where(y == q, x[:128], x[128:])
        return jnp.where(c == 0, x, jnp.concatenate([x[64:], x[:64]], axis=0))

    straight = jnp.where(low_i, half(from0, 0), half(from1, 1))
    crossed = jnp.where(low_i, half(from0, 1), half(from1, 0))
    solved = (straight + roll(crossed)).astype(BF)
    both = jnp.concatenate(
        [jnp.where(low_i, solved, zero), jnp.where(low_i, zero, solved)], axis=0
    )
    answers = dot(select, both).astype(BF).reshape(32, 32, 384)
    back = lax.all_to_all(answers, EXCHANGE, 0, 0, tiled=True).reshape(4, 256, 384)
    total = finish(weights, back, pick, *spread, eliminated)
    pieces = lax.all_to_all(total.reshape(8, 128, 384), SHIFT, 0, 0, tiled=True)
    return jnp.sum(pieces.reshape(8, 128, 1, 384).astype(F32), axis=0)


def solution(mesh):
    fine = Mesh(mesh.devices.reshape(2, 4, 2, 8, 2), ("yl", "x", "yh", "z", "c"))
    in_specs = (
        P(SUB, None, None),
        P(),
        P(SHIFT, SUB, None, None),
        P(SUB, None, None),
        P(SHIFT, SUB, None),
        P(SHIFT),
        P(),
        P(),
    )
    out_specs = P(SHIFT, SUB, None)

    return jax.shard_map(
        on_device, mesh=fine, in_specs=in_specs, out_specs=out_specs, check_vma=False
    )
```

```python
import jax
import jax.numpy as jnp
from jax import lax
from jax.experimental import pallas as pl
from jax.experimental.pallas import tpu as pltpu
from jax.sharding import Mesh, PartitionSpec as P

BF = jnp.bfloat16
F32 = jnp.float32
SUB = ("yh", "z", "c")
EXCHANGE = ("yh", "c", "z")
SHIFT = ("yl", "x")
HALF = 192


def dot(a, b):
    return jnp.dot(a, b, preferred_element_type=F32)


def dot_t(a, b):
    return lax.dot_general(a, b, (((0,), (0,)), ((), ())), preferred_element_type=F32)


def roll(a):
    return jnp.concatenate([a[:, HALF:], a[:, :HALF]], axis=1)


def roll32(a):
    return pltpu.roll(a, HALF, 1)


def start_kernel(
    position_ref,
    owner_ref,
    blocks_ref,
    inverse_ref,
    rhs_ref,
    couple_ref,
    eliminated_ref,
    packed_ref,
    pack_ref,
    pick_ref,
    total_ref,
):
    j, i = pl.program_id(0), pl.program_id(1)

    @pl.when((j == 0) & (i == 0))
    def _():
        row = blocks_ref[pl.ds(owner_ref[position_ref[0]], 1), :]
        across = jnp.broadcast_to(row, (256, 256))
        down = jnp.broadcast_to(row.astype(F32), (256, 256)).T.astype(jnp.int32)
        same = (across >> 6) == (down >> 6)
        rank = jnp.sum((same & (down < across)).astype(F32), axis=0, keepdims=True)
        slot = ((row >> 7) & 7) * 32 + ((row >> 6) & 1) * 16 + rank.astype(jnp.int32)
        hit = lax.broadcasted_iota(jnp.int32, (256, 256), 0) == slot
        pack_ref[:, :256] = jnp.where(hit & (across < 1024), 1.0, 0.0).astype(BF)
        pack_ref[:, 256:] = jnp.where(hit & (across >= 1024), 1.0, 0.0).astype(BF)
        rank = jnp.sum((same & (across < down)).astype(F32), axis=1, keepdims=True)
        slot = ((down >> 7) & 7) * 32 + ((down >> 6) & 1) * 16 + rank.astype(jnp.int32)
        hit = lax.broadcasted_iota(jnp.int32, (256, 256), 1) == slot
        pick_ref[:256] = jnp.where(hit & (down < 1024), 1.0, 0.0).astype(BF)
        pick_ref[256:] = jnp.where(hit & (down >= 1024), 1.0, 0.0).astype(BF)

    @pl.when(i == 0)
    def _():
        total_ref[...] = jnp.zeros_like(total_ref)

    part = dot(inverse_ref[0, 0], rhs_ref[0]).astype(BF)
    eliminated_ref[0] = part
    total_ref[...] += dot_t(couple_ref[0], part)

    @pl.when(i == pl.num_programs(1) - 1)
    def _():
        coupled = total_ref[...].astype(BF).astype(F32)
        turned = roll32(coupled)
        low = lax.broadcasted_iota(jnp.int32, (256, 384), 1) < HALF
        for h, (a, b) in enumerate(((coupled, turned), (turned, coupled))):
            a = jnp.where(low, a, 0.0).astype(BF)
            b = jnp.where(low, 0.0, b).astype(BF)
            packed_ref[h, 0] = (dot(pack_ref[:, :256], a) + dot(pack_ref[:, 256:], b)).astype(BF)


def start(position, owner_sub, index_blocks, inverse, rhs, couple, rows=1024):
    steps = 1024 // rows
    smem = pl.BlockSpec(memory_space=pltpu.SMEM)
    return pl.pallas_call(
        start_kernel,
        grid=(2, steps),
        in_specs=[
            smem,
            smem,
            pl.BlockSpec((32, 256), lambda j, i: (0, 0)),
            pl.BlockSpec((1, 1, rows, 1024), lambda j, i: (j, 0, i, 0)),
            pl.BlockSpec((1, 1024, 384), lambda j, i: (0, 0, 0)),
            pl.BlockSpec((1, rows, 256), lambda j, i: (0, i, 0)),
        ],
        out_specs=[
            pl.BlockSpec((1, rows, 384), lambda j, i: (j, i, 0)),
            pl.BlockSpec((2, 1, 256, 384), lambda j, i: (0, j, 0, 0)),
            pl.BlockSpec((256, 512), lambda j, i: (0, 0)),
            pl.BlockSpec((512, 256), lambda j, i: (0, 0)),
        ],
        out_shape=[
            jax.ShapeDtypeStruct((2, 1024, 384), BF),
            jax.ShapeDtypeStruct((2, 2, 256, 384), BF),
            jax.ShapeDtypeStruct((256, 512), BF),
            jax.ShapeDtypeStruct((512, 256), BF),
        ],
        scratch_shapes=[pltpu.VMEM((256, 384), F32)],
        name="start",
    )(position, owner_sub, index_blocks, inverse, rhs, couple)


CHUNK = 256
WHOLE = pl.BlockSpec(memory_space=pltpu.VMEM)
SCALAR = pl.BlockSpec(memory_space=pltpu.SMEM)


def solve_kernel(y_ref, z_ref, c_ref, *refs):
    blocks, rows = refs[:8], refs[8:12]
    select_ref, answers_ref, gathered_ref, schur_ref, both_ref = refs[12:]
    y, z, c = y_ref[0], z_ref[0], c_ref[0]
    for step, block in zip((0, -1, 1, -2, 2, -3, 3, 4), blocks):
        at = pl.multiple_of(((z + step + 8) & 7) * 128, 128)
        gathered_ref[pl.ds(at, 128)] = block[...]
    for (dy, dc), part in zip(((0, 0), (0, 1), (1, 0), (1, 1)), rows):
        at = pl.multiple_of(((y + dy) & 1) * 128 + ((c + dc) & 1) * 64, 64)
        schur_ref[pl.ds(at, 64)] = part[...]
    low = lax.broadcasted_iota(jnp.int32, (128, 384), 1) < HALF
    from0 = dot(schur_ref[:, :1024], gathered_ref[...])
    from1 = dot(schur_ref[:, 1024:], gathered_ref[...])
    straight = jnp.where(low, from0[:128], from1[128:])
    crossed = jnp.where(low, from0[128:], from1[:128])
    solved = straight + roll32(crossed)
    both_ref[:128] = jnp.where(low, solved, 0.0).astype(BF)
    both_ref[128:] = jnp.where(low, 0.0, solved).astype(BF)
    answers_ref[...] = dot(select_ref[...], both_ref[...]).astype(BF)


def solve(place, blocks, rows, select):
    return pl.pallas_call(
        solve_kernel,
        in_specs=[SCALAR] * 3 + [WHOLE] * 13,
        out_specs=WHOLE,
        out_shape=jax.ShapeDtypeStruct((1024, 384), BF),
        scratch_shapes=[
            pltpu.VMEM((1024, 384), BF),
            pltpu.VMEM((256, 2048), BF),
            pltpu.VMEM((256, 384), BF),
        ],
        compiler_params=pltpu.CompilerParams(vmem_limit_bytes=8 << 20),
        name="solve",
    )(*place, *blocks, *rows, select)


def finish_kernel(
    weights_ref, back_ref, pick_ref, spread0_ref, spread1_ref, eliminated_ref, out_ref, picked_ref
):
    low = lax.broadcasted_iota(jnp.int32, (256, 384), 1) < HALF
    for j in range(2):
        top = [dot(pick_ref[:256], back_ref[2 * h + j]) for h in range(2)]
        end = [dot(pick_ref[256:], back_ref[2 * h + j]) for h in range(2)]
        straight = jnp.where(low, top[0], end[1])
        crossed = jnp.where(low, top[1], end[0])
        picked_ref[j] = (straight + roll32(crossed)).astype(BF)
    for i in range(1024 // CHUNK):
        rows = pl.ds(i * CHUNK, CHUNK)
        total = weights_ref[0] * eliminated_ref[0, rows].astype(F32)
        total += weights_ref[1] * eliminated_ref[1, rows].astype(F32)
        total -= dot(spread0_ref[rows], picked_ref[0]) + dot(spread1_ref[rows], picked_ref[1])
        out_ref[rows] = total.astype(BF)


def finish(weights, back, pick, spread0, spread1, eliminated):
    return pl.pallas_call(
        finish_kernel,
        in_specs=[SCALAR] + [WHOLE] * 5,
        out_specs=WHOLE,
        out_shape=jax.ShapeDtypeStruct((1024, 384), BF),
        scratch_shapes=[pltpu.VMEM((2, 256, 384), BF)],
        compiler_params=pltpu.CompilerParams(vmem_limit_bytes=8 << 20),
        name="finish",
    )(weights, back, pick, spread0, spread1, eliminated)


def add_kernel(pieces_ref, out_ref):
    total = pieces_ref[0].astype(F32)
    for i in range(1, 8):
        total += pieces_ref[i].astype(F32)
    out_ref[...] = total[:, None, :]


def add(pieces):
    return pl.pallas_call(
        add_kernel,
        in_specs=[WHOLE],
        out_specs=WHOLE,
        out_shape=jax.ShapeDtypeStruct((128, 1, 384), F32),
        compiler_params=pltpu.CompilerParams(vmem_limit_bytes=4 << 20),
        name="add",
    )(pieces)


def on_device(
    interior_rhs,
    interface_rhs,
    interior_inverse,
    coupling,
    schur_inverse,
    weights,
    owner_sub,
    index_blocks,
):
    y, z, c = lax.axis_index("yh"), lax.axis_index("z"), lax.axis_index("c")
    swap = [(0, 1), (1, 0)]

    def low(shape):
        return lax.broadcasted_iota(jnp.int32, shape, len(shape) - 1) < HALF

    position = ((y * 8 + z) * 2 + c).astype(jnp.int32)
    eliminated, packed, _, pick = start(
        position[None], owner_sub, index_blocks, interior_inverse, interior_rhs, coupling
    )
    packed, schur_inverse = lax.optimization_barrier((packed, schur_inverse))
    packed = packed.reshape(32, 32, 384)
    arrived = lax.all_to_all(packed, EXCHANGE, 0, 0, tiled=True).reshape(1024, 384)

    keep = lax.dynamic_index_in_dim(schur_inverse, c, 0, keepdims=False)
    give = lax.dynamic_index_in_dim(schur_inverse, 1 - c, 0, keepdims=False)
    across = lax.ppermute(give, ("yh", "c"), [(0, 3), (1, 2), (2, 1), (3, 0)])
    beyond = lax.ppermute(keep, "yh", swap)
    beside = lax.ppermute(give, "c", swap)

    owners = owner_sub.reshape(2, 8, 2).transpose(0, 2, 1).reshape(32)
    names = lax.broadcasted_iota(jnp.int32, (32, 32, 1), 1)
    idx_all = jnp.sum(jnp.where(owners[:, None, None] == names, index_blocks[None], 0), axis=1)
    rows = lax.broadcasted_iota(jnp.int32, (1, 1, 256), 2)
    rows = (rows // 128) * 1024 + z * 128 + rows % 128
    held = jnp.any(idx_all[:, :, None] == rows, axis=1)
    first = lax.broadcasted_iota(jnp.int32, (256, 256), 0)
    second = lax.broadcasted_iota(jnp.int32, (256, 256), 1)
    before = ((first < second) & (first // 64 == second // 64)).astype(BF)
    place = dot(held.astype(BF), before).astype(jnp.int32)
    place = place + 16 * ((lax.broadcasted_iota(jnp.int32, (32, 256), 1) // 64) % 2)
    place = jnp.where(held, place, -1)
    select = (
        (place[:, None, :] == lax.broadcasted_iota(jnp.int32, (32, 32, 256), 1))
        .astype(BF)
        .reshape(1024, 256)
    )

    base = [lax.dynamic_slice_in_dim(interface_rhs, q * 1024 + z * 128, 128, 0) for q in range(2)]
    low_i = low((128, 384))
    plane_rhs = jnp.where(
        y == 0,
        jnp.where(low_i, base[0], roll(base[1])),
        jnp.where(low_i, roll(base[0]), base[1]),
    )

    spread = [(weights[j] * dot(interior_inverse[j, 0], coupling[0])).astype(BF) for j in range(2)]

    arrived, select, spread, plane_rhs = lax.optimization_barrier(
        (arrived, select, spread, plane_rhs)
    )

    summed = dot_t(select, arrived)
    summed = jnp.where(low_i, summed[:128], summed[128:])
    reduced = (plane_rhs.astype(F32) - summed).astype(BF)

    up = [(i, (i + 1) % 8) for i in range(8)]
    down = [(i, (i + 7) % 8) for i in range(8)]
    up2 = [(i, (i + 2) % 8) for i in range(8)]
    down2 = [(i, (i + 6) % 8) for i in range(8)]
    below2 = lax.ppermute(reduced, "z", up2)
    above2 = lax.ppermute(reduced, "z", down2)
    below1, above1 = lax.ppermute(reduced, "z", up), lax.ppermute(reduced, "z", down)
    opposite = lax.ppermute(below2, "z", up2)
    below3, above3 = lax.ppermute(below2, "z", up), lax.ppermute(above2, "z", down)
    answers = solve(
        [i.astype(jnp.int32)[None] for i in (y, z, c)],
        (reduced, below1, above1, below2, above2, below3, above3, opposite),
        (keep, beside, beyond, across),
        select,
    ).reshape(32, 32, 384)
    back = lax.all_to_all(answers, EXCHANGE, 0, 0, tiled=True).reshape(4, 256, 384)
    total = finish(weights, back, pick, *spread, eliminated)
    pieces = lax.all_to_all(total.reshape(8, 128, 384), SHIFT, 0, 0, tiled=True)
    return add(pieces)


def solution(mesh):
    fine = Mesh(mesh.devices.reshape(2, 4, 2, 8, 2), ("yl", "x", "yh", "z", "c"))
    in_specs = (
        P(SUB, None, None),
        P(),
        P(SHIFT, SUB, None, None),
        P(SUB, None, None),
        P(SHIFT, SUB, None),
        P(SHIFT),
        P(),
        P(),
    )
    out_specs = P(SHIFT, SUB, None)

    return jax.shard_map(
        on_device, mesh=fine, in_specs=in_specs, out_specs=out_specs, check_vma=False
    )
```

```python
import jax
import jax.numpy as jnp
from jax import lax
from jax.experimental import pallas as pl
from jax.experimental.pallas import tpu as pltpu
from jax.sharding import Mesh, PartitionSpec as P

BF = jnp.bfloat16
F32 = jnp.float32
SUB = ("yh", "z", "c")
EXCHANGE = ("yh", "c", "z")
SHIFT = ("yl", "x")
HALF = 192


def dot(a, b):
    return jnp.dot(a, b, preferred_element_type=F32)


def dot_t(a, b):
    return lax.dot_general(a, b, (((0,), (0,)), ((), ())), preferred_element_type=F32)


def roll(a):
    return jnp.concatenate([a[:, HALF:], a[:, :HALF]], axis=1)


def roll32(a):
    return pltpu.roll(a, HALF, 1)


def start_kernel(
    position_ref,
    owner_ref,
    blocks_ref,
    inverse_ref,
    rhs_ref,
    couple_ref,
    eliminated_ref,
    packed_ref,
    pick_ref,
    pack_ref,
    total_ref,
):
    j, i = pl.program_id(0), pl.program_id(1)

    @pl.when((j == 0) & (i == 0))
    def _():
        row = blocks_ref[pl.ds(owner_ref[position_ref[0]], 1), :]
        across = jnp.broadcast_to(row, (256, 256))
        down = jnp.broadcast_to(row.astype(F32), (256, 256)).T.astype(jnp.int32)
        same = (across >> 6) == (down >> 6)
        rank = jnp.sum((same & (down < across)).astype(F32), axis=0, keepdims=True)
        slot = ((row >> 7) & 7) * 32 + ((row >> 6) & 1) * 16 + rank.astype(jnp.int32)
        hit = lax.broadcasted_iota(jnp.int32, (256, 256), 0) == slot
        pack_ref[:, :256] = jnp.where(hit & (across < 1024), 1.0, 0.0).astype(BF)
        pack_ref[:, 256:] = jnp.where(hit & (across >= 1024), 1.0, 0.0).astype(BF)
        rank = jnp.sum((same & (across < down)).astype(F32), axis=1, keepdims=True)
        slot = ((down >> 7) & 7) * 32 + ((down >> 6) & 1) * 16 + rank.astype(jnp.int32)
        hit = lax.broadcasted_iota(jnp.int32, (256, 256), 1) == slot
        pick_ref[:256] = jnp.where(hit & (down < 1024), 1.0, 0.0).astype(BF)
        pick_ref[256:] = jnp.where(hit & (down >= 1024), 1.0, 0.0).astype(BF)

    @pl.when(i == 0)
    def _():
        total_ref[...] = jnp.zeros_like(total_ref)

    part = dot(inverse_ref[0, 0], rhs_ref[0]).astype(BF)
    eliminated_ref[0] = part
    total_ref[...] += dot_t(couple_ref[0], part)

    @pl.when(i == pl.num_programs(1) - 1)
    def _():
        coupled = total_ref[...].astype(BF).astype(F32)
        turned = roll32(coupled)
        low = lax.broadcasted_iota(jnp.int32, (256, 384), 1) < HALF
        for h, (a, b) in enumerate(((coupled, turned), (turned, coupled))):
            a = jnp.where(low, a, 0.0).astype(BF)
            b = jnp.where(low, 0.0, b).astype(BF)
            packed_ref[h, 0] = (dot(pack_ref[:, :256], a) + dot(pack_ref[:, 256:], b)).astype(BF)


def start(position, owner_sub, index_blocks, inverse, rhs, couple, rows=1024):
    steps = 1024 // rows
    smem = pl.BlockSpec(memory_space=pltpu.SMEM)
    return pl.pallas_call(
        start_kernel,
        grid=(2, steps),
        in_specs=[
            smem,
            smem,
            pl.BlockSpec((32, 256), lambda j, i: (0, 0)),
            pl.BlockSpec((1, 1, rows, 1024), lambda j, i: (j, 0, i, 0)),
            pl.BlockSpec((1, 1024, 384), lambda j, i: (0, 0, 0)),
            pl.BlockSpec((1, rows, 256), lambda j, i: (0, i, 0)),
        ],
        out_specs=[
            pl.BlockSpec((1, rows, 384), lambda j, i: (j, i, 0)),
            pl.BlockSpec((2, 1, 256, 384), lambda j, i: (0, j, 0, 0)),
            pl.BlockSpec((512, 256), lambda j, i: (0, 0)),
        ],
        out_shape=[
            jax.ShapeDtypeStruct((2, 1024, 384), BF),
            jax.ShapeDtypeStruct((2, 2, 256, 384), BF),
            jax.ShapeDtypeStruct((512, 256), BF),
        ],
        scratch_shapes=[pltpu.VMEM((256, 512), BF), pltpu.VMEM((256, 384), F32)],
        name="start",
    )(position, owner_sub, index_blocks, inverse, rhs, couple)


CHUNK = 256
WHOLE = pl.BlockSpec(memory_space=pltpu.VMEM)
SCALAR = pl.BlockSpec(memory_space=pltpu.SMEM)


def solve_kernel(y_ref, z_ref, c_ref, *refs):
    blocks, rows = refs[:8], refs[8:12]
    select_ref, answers_ref, gathered_ref, schur_ref, both_ref = refs[12:]
    y, z, c = y_ref[0], z_ref[0], c_ref[0]
    for step, block in zip((0, -1, 1, -2, 2, -3, 3, 4), blocks):
        at = pl.multiple_of(((z + step + 8) & 7) * 128, 128)
        gathered_ref[pl.ds(at, 128)] = block[...]
    for (dy, dc), part in zip(((0, 0), (0, 1), (1, 0), (1, 1)), rows):
        at = pl.multiple_of(((y + dy) & 1) * 128 + ((c + dc) & 1) * 64, 64)
        schur_ref[pl.ds(at, 64)] = part[...]
    low = lax.broadcasted_iota(jnp.int32, (128, 384), 1) < HALF
    from0 = dot(schur_ref[:, :1024], gathered_ref[...])
    from1 = dot(schur_ref[:, 1024:], gathered_ref[...])
    straight = jnp.where(low, from0[:128], from1[128:])
    crossed = jnp.where(low, from0[128:], from1[:128])
    solved = straight + roll32(crossed)
    both_ref[:128] = jnp.where(low, solved, 0.0).astype(BF)
    both_ref[128:] = jnp.where(low, 0.0, solved).astype(BF)
    answers_ref[...] = dot(select_ref[...], both_ref[...]).astype(BF)


def solve(place, blocks, rows, select):
    return pl.pallas_call(
        solve_kernel,
        in_specs=[SCALAR] * 3 + [WHOLE] * 13,
        out_specs=WHOLE,
        out_shape=jax.ShapeDtypeStruct((1024, 384), BF),
        scratch_shapes=[
            pltpu.VMEM((1024, 384), BF),
            pltpu.VMEM((256, 2048), BF),
            pltpu.VMEM((256, 384), BF),
        ],
        compiler_params=pltpu.CompilerParams(vmem_limit_bytes=8 << 20),
        name="solve",
    )(*place, *blocks, *rows, select)


def finish_kernel(
    weights_ref, back_ref, pick_ref, spread0_ref, spread1_ref, eliminated_ref, out_ref, picked_ref
):
    low = lax.broadcasted_iota(jnp.int32, (256, 384), 1) < HALF
    for j in range(2):
        top = [dot(pick_ref[:256], back_ref[2 * h + j]) for h in range(2)]
        end = [dot(pick_ref[256:], back_ref[2 * h + j]) for h in range(2)]
        straight = jnp.where(low, top[0], end[1])
        crossed = jnp.where(low, top[1], end[0])
        picked_ref[j] = (straight + roll32(crossed)).astype(BF)
    for i in range(1024 // CHUNK):
        rows = pl.ds(i * CHUNK, CHUNK)
        total = weights_ref[0] * eliminated_ref[0, rows].astype(F32)
        total += weights_ref[1] * eliminated_ref[1, rows].astype(F32)
        total -= dot(spread0_ref[rows], picked_ref[0]) + dot(spread1_ref[rows], picked_ref[1])
        total = total.astype(BF)
        for b in range(CHUNK // 128):
            yl, x = divmod(i * CHUNK // 128 + b, 4)
            out_ref[pl.ds((2 * x + yl) * 128, 128)] = total[128 * b : 128 * b + 128]


def finish(weights, back, pick, spread0, spread1, eliminated):
    return pl.pallas_call(
        finish_kernel,
        in_specs=[SCALAR] + [WHOLE] * 5,
        out_specs=WHOLE,
        out_shape=jax.ShapeDtypeStruct((1024, 384), BF),
        scratch_shapes=[pltpu.VMEM((2, 256, 384), BF)],
        compiler_params=pltpu.CompilerParams(vmem_limit_bytes=8 << 20),
        name="finish",
    )(weights, back, pick, spread0, spread1, eliminated)


def add_kernel(pieces_ref, out_ref):
    total = pieces_ref[0].astype(F32)
    for i in range(1, 8):
        total += pieces_ref[i].astype(F32)
    out_ref[...] = total[:, None, :]


def add(pieces):
    return pl.pallas_call(
        add_kernel,
        in_specs=[WHOLE],
        out_specs=WHOLE,
        out_shape=jax.ShapeDtypeStruct((128, 1, 384), F32),
        compiler_params=pltpu.CompilerParams(vmem_limit_bytes=4 << 20),
        name="add",
    )(pieces)


def on_device(
    interior_rhs,
    interface_rhs,
    interior_inverse,
    coupling,
    schur_inverse,
    weights,
    owner_sub,
    index_blocks,
):
    y, z, c = lax.axis_index("yh"), lax.axis_index("z"), lax.axis_index("c")
    swap = [(0, 1), (1, 0)]

    def low(shape):
        return lax.broadcasted_iota(jnp.int32, shape, len(shape) - 1) < HALF

    position = ((y * 8 + z) * 2 + c).astype(jnp.int32)
    eliminated, packed, pick = start(
        position[None], owner_sub, index_blocks, interior_inverse, interior_rhs, coupling
    )
    packed, schur_inverse = lax.optimization_barrier((packed, schur_inverse))
    packed = packed.reshape(32, 32, 384)
    arrived = lax.all_to_all(packed, EXCHANGE, 0, 0, tiled=True).reshape(1024, 384)

    keep = lax.dynamic_index_in_dim(schur_inverse, c, 0, keepdims=False)
    give = lax.dynamic_index_in_dim(schur_inverse, 1 - c, 0, keepdims=False)
    across = lax.ppermute(give, ("yh", "c"), [(0, 3), (1, 2), (2, 1), (3, 0)])
    beyond = lax.ppermute(keep, "yh", swap)
    beside = lax.ppermute(give, "c", swap)

    owners = owner_sub.reshape(2, 8, 2).transpose(0, 2, 1).reshape(32)
    names = lax.broadcasted_iota(jnp.int32, (32, 32, 1), 1)
    idx_all = jnp.sum(jnp.where(owners[:, None, None] == names, index_blocks[None], 0), axis=1)
    rows = lax.broadcasted_iota(jnp.int32, (1, 1, 256), 2)
    rows = (rows // 128) * 1024 + z * 128 + rows % 128
    held = jnp.any(idx_all[:, :, None] == rows, axis=1)
    first = lax.broadcasted_iota(jnp.int32, (256, 256), 0)
    second = lax.broadcasted_iota(jnp.int32, (256, 256), 1)
    before = ((first < second) & (first // 64 == second // 64)).astype(BF)
    place = dot(held.astype(BF), before).astype(jnp.int32)
    place = place + 16 * ((lax.broadcasted_iota(jnp.int32, (32, 256), 1) // 64) % 2)
    place = jnp.where(held, place, -1)
    select = (
        (place[:, None, :] == lax.broadcasted_iota(jnp.int32, (32, 32, 256), 1))
        .astype(BF)
        .reshape(1024, 256)
    )

    base = [lax.dynamic_slice_in_dim(interface_rhs, q * 1024 + z * 128, 128, 0) for q in range(2)]
    low_i = low((128, 384))
    plane_rhs = jnp.where(
        y == 0,
        jnp.where(low_i, base[0], roll(base[1])),
        jnp.where(low_i, roll(base[0]), base[1]),
    )

    spread = [(weights[j] * dot(interior_inverse[j, 0], coupling[0])).astype(BF) for j in range(2)]

    arrived, select, spread, plane_rhs = lax.optimization_barrier(
        (arrived, select, spread, plane_rhs)
    )

    summed = dot_t(select, arrived)
    summed = jnp.where(low_i, summed[:128], summed[128:])
    reduced = (plane_rhs.astype(F32) - summed).astype(BF)

    up = [(i, (i + 1) % 8) for i in range(8)]
    down = [(i, (i + 7) % 8) for i in range(8)]
    up2 = [(i, (i + 2) % 8) for i in range(8)]
    down2 = [(i, (i + 6) % 8) for i in range(8)]
    below2 = lax.ppermute(reduced, "z", up2)
    above2 = lax.ppermute(reduced, "z", down2)
    below1, above1 = lax.ppermute(reduced, "z", up), lax.ppermute(reduced, "z", down)
    opposite = lax.ppermute(below2, "z", up2)
    below3, above3 = lax.ppermute(below2, "z", up), lax.ppermute(above2, "z", down)
    answers = solve(
        [i.astype(jnp.int32)[None] for i in (y, z, c)],
        (reduced, below1, above1, below2, above2, below3, above3, opposite),
        (keep, beside, beyond, across),
        select,
    ).reshape(32, 32, 384)
    back = lax.all_to_all(answers, EXCHANGE, 0, 0, tiled=True).reshape(4, 256, 384)
    total = finish(weights, back, pick, *spread, eliminated)
    pieces = lax.all_to_all(total.reshape(8, 128, 384), ("x", "yl"), 0, 0, tiled=True)
    return add(pieces)


def solution(mesh):
    fine = Mesh(mesh.devices.reshape(2, 4, 2, 8, 2), ("yl", "x", "yh", "z", "c"))
    in_specs = (
        P(SUB, None, None),
        P(),
        P(SHIFT, SUB, None, None),
        P(SUB, None, None),
        P(SHIFT, SUB, None),
        P(SHIFT),
        P(),
        P(),
    )
    out_specs = P(SHIFT, SUB, None)

    return jax.shard_map(
        on_device, mesh=fine, in_specs=in_specs, out_specs=out_specs, check_vma=False
    )
```

```python
import jax
import jax.numpy as jnp
from jax import lax
from jax.experimental import pallas as pl
from jax.experimental.pallas import tpu as pltpu
from jax.sharding import Mesh, PartitionSpec as P

BF = jnp.bfloat16
F32 = jnp.float32
SUB = ("yh", "z", "c")
EXCHANGE = ("yh", "c", "z")
SHIFT = ("yl", "x")
HALF = 192


def dot(a, b):
    return jnp.dot(a, b, preferred_element_type=F32)


def dot_t(a, b):
    return lax.dot_general(a, b, (((0,), (0,)), ((), ())), preferred_element_type=F32)


def roll(a):
    return jnp.concatenate([a[:, HALF:], a[:, :HALF]], axis=1)


def roll32(a):
    return pltpu.roll(a, HALF, 1)


def start_kernel(
    position_ref,
    owner_ref,
    blocks_ref,
    inverse_ref,
    rhs_ref,
    couple_hbm,
    eliminated_ref,
    packed_ref,
    pick_ref,
    pack_ref,
    total_ref,
    couple_ref,
    sem,
):
    j, i = pl.program_id(0), pl.program_id(1)
    fetch = pltpu.make_async_copy(couple_hbm, couple_ref, sem)

    @pl.when((j == 0) & (i == 0))
    def _():
        fetch.start()

    @pl.when((j == 0) & (i == 0))
    def _():
        row = blocks_ref[pl.ds(owner_ref[position_ref[0]], 1), :]
        across = jnp.broadcast_to(row, (256, 256))
        down = jnp.broadcast_to(row.astype(F32), (256, 256)).T.astype(jnp.int32)
        same = (across >> 6) == (down >> 6)
        rank = jnp.sum((same & (down < across)).astype(F32), axis=0, keepdims=True)
        slot = ((row >> 7) & 7) * 32 + ((row >> 6) & 1) * 16 + rank.astype(jnp.int32)
        hit = lax.broadcasted_iota(jnp.int32, (256, 256), 0) == slot
        pack_ref[:, :256] = jnp.where(hit & (across < 1024), 1.0, 0.0).astype(BF)
        pack_ref[:, 256:] = jnp.where(hit & (across >= 1024), 1.0, 0.0).astype(BF)
        rank = jnp.sum((same & (across < down)).astype(F32), axis=1, keepdims=True)
        slot = ((down >> 7) & 7) * 32 + ((down >> 6) & 1) * 16 + rank.astype(jnp.int32)
        hit = lax.broadcasted_iota(jnp.int32, (256, 256), 1) == slot
        pick_ref[:256] = jnp.where(hit & (down < 1024), 1.0, 0.0).astype(BF)
        pick_ref[256:] = jnp.where(hit & (down >= 1024), 1.0, 0.0).astype(BF)

    @pl.when(i == 0)
    def _():
        total_ref[...] = jnp.zeros_like(total_ref)

    part = dot(inverse_ref[0, 0], rhs_ref[0]).astype(BF)
    eliminated_ref[0] = part

    @pl.when((j == 0) & (i == 0))
    def _():
        fetch.wait()

    total_ref[...] += dot_t(couple_ref[0, pl.ds(i * part.shape[0], part.shape[0])], part)

    @pl.when(i == pl.num_programs(1) - 1)
    def _():
        coupled = total_ref[...].astype(BF).astype(F32)
        turned = roll32(coupled)
        low = lax.broadcasted_iota(jnp.int32, (256, 384), 1) < HALF
        for h, (a, b) in enumerate(((coupled, turned), (turned, coupled))):
            a = jnp.where(low, a, 0.0).astype(BF)
            b = jnp.where(low, 0.0, b).astype(BF)
            packed_ref[h, 0] = (dot(pack_ref[:, :256], a) + dot(pack_ref[:, 256:], b)).astype(BF)


def start(position, owner_sub, index_blocks, inverse, rhs, couple, rows=1024):
    steps = 1024 // rows
    smem = pl.BlockSpec(memory_space=pltpu.SMEM)
    return pl.pallas_call(
        start_kernel,
        grid=(2, steps),
        in_specs=[
            smem,
            smem,
            pl.BlockSpec((32, 256), lambda j, i: (0, 0)),
            pl.BlockSpec((1, 1, rows, 1024), lambda j, i: (j, 0, i, 0)),
            pl.BlockSpec((1, 1024, 384), lambda j, i: (0, 0, 0)),
            pl.BlockSpec(memory_space=pl.ANY),
        ],
        out_specs=[
            pl.BlockSpec((1, rows, 384), lambda j, i: (j, i, 0)),
            pl.BlockSpec((2, 1, 256, 384), lambda j, i: (0, j, 0, 0)),
            pl.BlockSpec((512, 256), lambda j, i: (0, 0)),
        ],
        out_shape=[
            jax.ShapeDtypeStruct((2, 1024, 384), BF),
            jax.ShapeDtypeStruct((2, 2, 256, 384), BF),
            jax.ShapeDtypeStruct((512, 256), BF),
        ],
        scratch_shapes=[
            pltpu.VMEM((256, 512), BF),
            pltpu.VMEM((256, 384), F32),
            pltpu.VMEM((1, 1024, 256), BF),
            pltpu.SemaphoreType.DMA,
        ],
        name="start",
    )(position, owner_sub, index_blocks, inverse, rhs, couple)


CHUNK = 256
WHOLE = pl.BlockSpec(memory_space=pltpu.VMEM)
SCALAR = pl.BlockSpec(memory_space=pltpu.SMEM)


def solve_kernel(y_ref, z_ref, c_ref, *refs):
    blocks, rows = refs[:8], refs[8:12]
    select_ref, answers_ref, gathered_ref, schur_ref, both_ref = refs[12:]
    y, z, c = y_ref[0], z_ref[0], c_ref[0]
    for step, block in zip((0, -1, 1, -2, 2, -3, 3, 4), blocks):
        at = pl.multiple_of(((z + step + 8) & 7) * 128, 128)
        gathered_ref[pl.ds(at, 128)] = block[...]
    for (dy, dc), part in zip(((0, 0), (0, 1), (1, 0), (1, 1)), rows):
        at = pl.multiple_of(((y + dy) & 1) * 128 + ((c + dc) & 1) * 64, 64)
        schur_ref[pl.ds(at, 64)] = part[...]
    low = lax.broadcasted_iota(jnp.int32, (128, 384), 1) < HALF
    from0 = dot(schur_ref[:, :1024], gathered_ref[...])
    from1 = dot(schur_ref[:, 1024:], gathered_ref[...])
    straight = jnp.where(low, from0[:128], from1[128:])
    crossed = jnp.where(low, from0[128:], from1[:128])
    solved = straight + roll32(crossed)
    both_ref[:128] = jnp.where(low, solved, 0.0).astype(BF)
    both_ref[128:] = jnp.where(low, 0.0, solved).astype(BF)
    answers_ref[...] = dot(select_ref[...], both_ref[...]).astype(BF)


def solve(place, blocks, rows, select):
    return pl.pallas_call(
        solve_kernel,
        in_specs=[SCALAR] * 3 + [WHOLE] * 13,
        out_specs=WHOLE,
        out_shape=jax.ShapeDtypeStruct((1024, 384), BF),
        scratch_shapes=[
            pltpu.VMEM((1024, 384), BF),
            pltpu.VMEM((256, 2048), BF),
            pltpu.VMEM((256, 384), BF),
        ],
        compiler_params=pltpu.CompilerParams(vmem_limit_bytes=8 << 20),
        name="solve",
    )(*place, *blocks, *rows, select)


def finish_kernel(
    weights_ref, back_ref, pick_ref, spread0_ref, spread1_ref, eliminated_ref, out_ref, picked_ref
):
    low = lax.broadcasted_iota(jnp.int32, (256, 384), 1) < HALF
    for j in range(2):
        top = [dot(pick_ref[:256], back_ref[2 * h + j]) for h in range(2)]
        end = [dot(pick_ref[256:], back_ref[2 * h + j]) for h in range(2)]
        straight = jnp.where(low, top[0], end[1])
        crossed = jnp.where(low, top[1], end[0])
        picked_ref[j] = (straight + roll32(crossed)).astype(BF)
    for i in range(1024 // CHUNK):
        rows = pl.ds(i * CHUNK, CHUNK)
        total = weights_ref[0] * eliminated_ref[0, rows].astype(F32)
        total += weights_ref[1] * eliminated_ref[1, rows].astype(F32)
        total -= dot(spread0_ref[rows], picked_ref[0]) + dot(spread1_ref[rows], picked_ref[1])
        total = total.astype(BF)
        for b in range(CHUNK // 128):
            yl, x = divmod(i * CHUNK // 128 + b, 4)
            out_ref[pl.ds((2 * x + yl) * 128, 128)] = total[128 * b : 128 * b + 128]


def finish(weights, back, pick, spread0, spread1, eliminated):
    return pl.pallas_call(
        finish_kernel,
        in_specs=[SCALAR] + [WHOLE] * 5,
        out_specs=WHOLE,
        out_shape=jax.ShapeDtypeStruct((1024, 384), BF),
        scratch_shapes=[pltpu.VMEM((2, 256, 384), BF)],
        compiler_params=pltpu.CompilerParams(vmem_limit_bytes=8 << 20),
        name="finish",
    )(weights, back, pick, spread0, spread1, eliminated)


def add_kernel(pieces_ref, out_ref):
    total = pieces_ref[0].astype(F32)
    for i in range(1, 8):
        total += pieces_ref[i].astype(F32)
    out_ref[...] = total[:, None, :]


def add(pieces):
    return pl.pallas_call(
        add_kernel,
        in_specs=[WHOLE],
        out_specs=WHOLE,
        out_shape=jax.ShapeDtypeStruct((128, 1, 384), F32),
        compiler_params=pltpu.CompilerParams(vmem_limit_bytes=4 << 20),
        name="add",
    )(pieces)


def on_device(
    interior_rhs,
    interface_rhs,
    interior_inverse,
    coupling,
    schur_inverse,
    weights,
    owner_sub,
    index_blocks,
):
    y, z, c = lax.axis_index("yh"), lax.axis_index("z"), lax.axis_index("c")
    swap = [(0, 1), (1, 0)]

    def low(shape):
        return lax.broadcasted_iota(jnp.int32, shape, len(shape) - 1) < HALF

    position = ((y * 8 + z) * 2 + c).astype(jnp.int32)
    eliminated, packed, pick = start(
        position[None], owner_sub, index_blocks, interior_inverse, interior_rhs, coupling
    )
    packed, schur_inverse = lax.optimization_barrier((packed, schur_inverse))
    packed = packed.reshape(32, 32, 384)
    arrived = lax.all_to_all(packed, EXCHANGE, 0, 0, tiled=True).reshape(1024, 384)

    keep = lax.dynamic_index_in_dim(schur_inverse, c, 0, keepdims=False)
    give = lax.dynamic_index_in_dim(schur_inverse, 1 - c, 0, keepdims=False)
    across = lax.ppermute(give, ("yh", "c"), [(0, 3), (1, 2), (2, 1), (3, 0)])
    beyond = lax.ppermute(keep, "yh", swap)
    beside = lax.ppermute(give, "c", swap)

    owners = owner_sub.reshape(2, 8, 2).transpose(0, 2, 1).reshape(32)
    names = lax.broadcasted_iota(jnp.int32, (32, 32, 1), 1)
    idx_all = jnp.sum(jnp.where(owners[:, None, None] == names, index_blocks[None], 0), axis=1)
    rows = lax.broadcasted_iota(jnp.int32, (1, 1, 256), 2)
    rows = (rows // 128) * 1024 + z * 128 + rows % 128
    held = jnp.any(idx_all[:, :, None] == rows, axis=1)
    first = lax.broadcasted_iota(jnp.int32, (256, 256), 0)
    second = lax.broadcasted_iota(jnp.int32, (256, 256), 1)
    before = ((first < second) & (first // 64 == second // 64)).astype(BF)
    place = dot(held.astype(BF), before).astype(jnp.int32)
    place = place + 16 * ((lax.broadcasted_iota(jnp.int32, (32, 256), 1) // 64) % 2)
    place = jnp.where(held, place, -1)
    select = (
        (place[:, None, :] == lax.broadcasted_iota(jnp.int32, (32, 32, 256), 1))
        .astype(BF)
        .reshape(1024, 256)
    )

    base = [lax.dynamic_slice_in_dim(interface_rhs, q * 1024 + z * 128, 128, 0) for q in range(2)]
    low_i = low((128, 384))
    plane_rhs = jnp.where(
        y == 0,
        jnp.where(low_i, base[0], roll(base[1])),
        jnp.where(low_i, roll(base[0]), base[1]),
    )

    spread = [(weights[j] * dot(interior_inverse[j, 0], coupling[0])).astype(BF) for j in range(2)]

    arrived, select, spread, plane_rhs = lax.optimization_barrier(
        (arrived, select, spread, plane_rhs)
    )

    summed = dot_t(select, arrived)
    summed = jnp.where(low_i, summed[:128], summed[128:])
    reduced = (plane_rhs.astype(F32) - summed).astype(BF)

    up = [(i, (i + 1) % 8) for i in range(8)]
    down = [(i, (i + 7) % 8) for i in range(8)]
    up2 = [(i, (i + 2) % 8) for i in range(8)]
    down2 = [(i, (i + 6) % 8) for i in range(8)]
    below2 = lax.ppermute(reduced, "z", up2)
    above2 = lax.ppermute(reduced, "z", down2)
    below1, above1 = lax.ppermute(reduced, "z", up), lax.ppermute(reduced, "z", down)
    opposite = lax.ppermute(below2, "z", up2)
    below3, above3 = lax.ppermute(below2, "z", up), lax.ppermute(above2, "z", down)
    answers = solve(
        [i.astype(jnp.int32)[None] for i in (y, z, c)],
        (reduced, below1, above1, below2, above2, below3, above3, opposite),
        (keep, beside, beyond, across),
        select,
    ).reshape(32, 32, 384)
    back = lax.all_to_all(answers, EXCHANGE, 0, 0, tiled=True).reshape(4, 256, 384)
    total = finish(weights, back, pick, *spread, eliminated)
    pieces = lax.all_to_all(total.reshape(8, 128, 384), ("x", "yl"), 0, 0, tiled=True)
    return add(pieces)


def solution(mesh):
    fine = Mesh(mesh.devices.reshape(2, 4, 2, 8, 2), ("yl", "x", "yh", "z", "c"))
    in_specs = (
        P(SUB, None, None),
        P(),
        P(SHIFT, SUB, None, None),
        P(SUB, None, None),
        P(SHIFT, SUB, None),
        P(SHIFT),
        P(),
        P(),
    )
    out_specs = P(SHIFT, SUB, None)

    return jax.shard_map(
        on_device, mesh=fine, in_specs=in_specs, out_specs=out_specs, check_vma=False
    )
```
